32 devices in a mesh: groups: 2 (over y), seq: 4 (over z), blk: 2 (over x), chan: 2 (over core).
Axes of the slice: x: 2, y: 2, z: 4, core: 2. Of those that a mesh axis runs over, the one named last changes fastest.
Arguments:
- queries: bfloat16 [4, 8, 32, 4096], P(('groups', 'blk'), 'seq', 'chan'), parts along dimension 0, may hold values from -8 to 8
- keys: bfloat16 [4, 8, 32, 4096], P(('groups', 'blk'), 'seq', 'chan'), parts along dimension 0, may hold values from -8 to 8
- values: bfloat16 [4, 8, 32, 4096], P(('groups', 'blk'), 'seq', 'chan'), parts along dimension 0, may hold values from -16 to 16
- norm_gain: float32 [4096], replicated, may hold values from 0.1 to 1.9
- head_weight: bfloat16 [4096, 64], replicated, may hold values from -0.09375 to 0.09375
- head_bias: float32 [64], replicated, may hold values from -3 to 3
- in_weight: bfloat16 [3, 3, 64, 512], replicated, may hold values from -0.25 to 0.25
- in_bias: float32 [512], replicated, may hold values from -3 to 3
- conv_weight: bfloat16 [3, 3, 512, 512], P(None, None, None, 'chan'), may hold values from -0.15625 to 0.15625
- conv_bias: float32 [512], P('chan'), may hold values from -3 to 3
Outputs:
- decoded: bfloat16 [4, 8, 32, 512], P(('groups', 'blk'), 'seq', None, 'chan'), parts along dimension 0
The draws below stay inside these ranges and needn't reach their ends.
There are 2 independent parts, one for each index of `groups`. The reference program is written for one: setup_inputs(seed, part) draws one part's arguments, and reference() takes and returns one part's arrays. A program takes and returns all parts, laid end to end along the dimension named above; an argument that names none is the same for every part. Nothing has to cross between parts.
All inputs are finite; a program needn't handle non-finite values.
Results may differ from the reference program's by a relative error of at most 0.025.
Values may be sent and summed in bfloat16 or wider, within the bound.
A program may use at most 64 MiB of HBM per device.

```python
import jax
import jax.numpy as jnp
from jax import lax

HD = 128
HEADS = 32
LAT = 64
WIDE = 512
COLS = 32
FEAT = 4096
FRAMES = 2
ROWS = 8


def shared_draw(key):
    key_query, key_keys = jax.random.split(jax.random.fold_in(key, 7), 2)
    token_count = FRAMES * ROWS * COLS
    shape = (token_count, FEAT)
    query_rows = jnp.clip(jax.random.normal(key_query, shape, jnp.float32), -8.0, 8.0)
    key_rows = jnp.clip(jax.random.normal(key_keys, shape, jnp.float32), -8.0, 8.0)
    return (query_rows.reshape(FRAMES, ROWS, COLS, FEAT), key_rows.reshape(FRAMES, ROWS, COLS, FEAT))


def draw_queries(key, part):
    return shared_draw(key)[0].astype(jnp.bfloat16)


def draw_keys(key, part):
    return shared_draw(key)[1].astype(jnp.bfloat16)


def draw_values(key, part):
    key_main = jax.random.fold_in(jax.random.fold_in(key, 11), 0)
    token_count = FRAMES * ROWS * COLS
    base = jax.random.normal(key_main, (token_count, HEADS, HD), jnp.float32)
    head_scale = 3.0 ** (jnp.arange(HEADS, dtype=jnp.float32) / max(HEADS - 1, 1))
    drawn = base * head_scale[None, :, None]
    drawn = jnp.clip(drawn, -16.0, 16.0)
    return drawn.reshape(FRAMES, ROWS, COLS, FEAT).astype(jnp.bfloat16)


def shard_levels(stream_key, dims, shards, smallest, high):
    loudness = 1.0
    for dim, shards_of in shards:
        draws = jax.random.uniform(jax.random.fold_in(jax.random.fold_in(stream_key, 6), dim), (shards_of,), jnp.float32, smallest / len(shards), high / len(shards))
        loudness = loudness * jnp.repeat(jnp.exp(draws), dims[dim] // shards_of).reshape((-1,) + (1,) * (len(dims) - 1 - dim))
    return loudness


def normal_values(stream_key, shape, width, reach, cuts=(), kind=jnp.bfloat16):
    gain = shard_levels(stream_key, shape, cuts, -0.22, 0.18) if cuts else 1.0
    values = jax.random.normal(stream_key, shape, jnp.float32) * width * gain
    return jnp.minimum(jnp.maximum(values, -reach), reach).astype(kind)


def setup_inputs(seed: int = 0, part: int = 0) -> dict:
    seeds = jax.random.split(jax.random.key(seed), 11)
    part_splits = jax.random.split(jax.random.fold_in(seeds[10], part), 11)
    return {
        "queries": draw_queries(jax.random.fold_in(jax.random.fold_in(seeds[10], part), 71), part),
        "keys": draw_keys(jax.random.fold_in(jax.random.fold_in(seeds[10], part), 71), part),
        "values": draw_values(jax.random.fold_in(jax.random.fold_in(seeds[10], part), 71), part),
        "norm_gain": jnp.clip(1.0 + 0.18 * jax.random.normal(seeds[3], (FEAT,), jnp.float32), 0.1, 1.9),
        "head_weight": normal_values(seeds[4], (FEAT, LAT), FEAT ** -0.5, 0.09375),
        "head_bias": normal_values(seeds[5], (LAT,), 0.5, 3.0, (), jnp.float32),
        "in_weight": normal_values(seeds[6], (3, 3, LAT, WIDE), (9 * LAT) ** -0.5, 0.25),
        "in_bias": normal_values(seeds[7], (WIDE,), 0.5, 3.0, (), jnp.float32),
        "conv_weight": normal_values(seeds[8], (3, 3, WIDE, WIDE), (3 * WIDE) ** -0.5, 0.15625, ((3, 2),)),
        "conv_bias": normal_values(seeds[9], (WIDE,), 0.5, 3.0, ((0, 2),), jnp.float32),
    }


epsilon = 1e-06

def conv_frame(inputs, kernel):
    padded = jnp.pad(inputs, ((0, 0), (1, 1), (1, 1), (0, 0)))
    frame_count, row_count, col_count, _ = inputs.shape
    result = jnp.zeros((frame_count * row_count * col_count, kernel.shape[3]), jnp.float32)
    for row_tap in range(3):
        for col_tap in range(3):
            window = padded[:, row_tap:row_tap + row_count, col_tap:col_tap + col_count, :]
            flat = window.reshape(-1, inputs.shape[3])
            result = result + jnp.dot(flat, kernel[row_tap, col_tap], preferred_element_type=jnp.float32)
    return result.reshape(frame_count, row_count, col_count, kernel.shape[3])

def reference(queries, keys, values, norm_gain, head_weight, head_bias, in_weight, in_bias, conv_weight, conv_bias):
    token_count = FRAMES * ROWS * COLS
    score_scale = HD ** (-0.5)
    query_heads = queries.reshape(token_count, HEADS, HD).transpose(1, 0, 2)
    key_heads = keys.reshape(token_count, HEADS, HD).transpose(1, 0, 2)
    value_heads = values.reshape(token_count, HEADS, HD).transpose(1, 0, 2)

    def one_head(triple):
        query_head, key_head, value_head = triple
        scores = jnp.dot(query_head, key_head.T, preferred_element_type=jnp.float32) * score_scale
        row_max = lax.optimization_barrier(jnp.max(scores, axis=-1, keepdims=True))
        expo = jnp.exp(scores - row_max)
        denoms = lax.optimization_barrier(jnp.sum(expo, axis=-1))
        numers = jnp.dot(expo.astype(jnp.bfloat16), value_head, preferred_element_type=jnp.float32)
        return (numers / denoms[:, None]).astype(jnp.bfloat16)
    attended = lax.map(one_head, (query_heads, key_heads, value_heads))
    attended = attended.transpose(1, 0, 2).reshape(token_count, FEAT)
    wide_att = attended.astype(jnp.float32)
    rms = jnp.sqrt(lax.optimization_barrier(jnp.mean(wide_att * wide_att, axis=-1)) + epsilon)
    normed = (wide_att * norm_gain).astype(jnp.bfloat16)
    projected = jnp.dot(normed, head_weight, preferred_element_type=jnp.float32)
    latent = (projected / rms[:, None] + head_bias).astype(jnp.bfloat16)
    latent = latent.reshape(FRAMES, ROWS, COLS, LAT)
    activation = jax.nn.silu(conv_frame(latent, in_weight) + in_bias).astype(jnp.bfloat16)
    decoded = (conv_frame(activation, conv_weight) + conv_bias).astype(jnp.bfloat16)
    return decoded
```

```python
import functools

import jax
import jax.numpy as jnp
from jax import lax
from jax.experimental import pallas as pl
from jax.experimental.pallas import tpu as pltpu
from jax.sharding import PartitionSpec as P

HD = 128
LOG2E = 1.4426950408889634
MESH = pl.DeviceIdType.MESH


epsilon = 1e-06


def with_halo(cells, sides, width):
    for axis, dim in sides:
        count = lax.axis_size(axis)
        ends = count - 1
        head = lax.slice_in_dim(cells, 0, width, axis=dim)
        tail = lax.slice_in_dim(cells, cells.shape[dim] - width, cells.shape[dim], axis=dim)
        cells = jnp.concatenate(
            [
                lax.ppermute(tail, axis, [(i, (i + 1) % count) for i in range(ends)]),
                cells,
                lax.ppermute(head, axis, [((i + 1) % count, i) for i in range(ends)]),
            ],
            axis=dim,
        )
    return cells


def conv_valid(inputs, kernel):
    col_count = inputs.shape[2]
    padded = jnp.pad(inputs, ((0, 0), (0, 0), (1, 1), (0, 0)))
    stacked = jnp.concatenate(
        [padded[:, :, col_tap : col_tap + col_count, :] for col_tap in range(3)], axis=-1
    )
    rows_out = inputs.shape[1] - 2
    result = None
    for row_tap in range(3):
        flat_kernel = kernel[row_tap].reshape(3 * kernel.shape[2], kernel.shape[3])
        term = jnp.einsum(
            "frci,io->frco",
            stacked[:, row_tap : row_tap + rows_out],
            flat_kernel,
            preferred_element_type=jnp.float32,
        )
        result = term if result is None else result + term
    return result


def absorb(running, key_block, value_block, query_heads, score_scale):
    run_max, denoms, numers = running
    scores = (
        jnp.einsum("hqd,hkd->hqk", query_heads, key_block, preferred_element_type=jnp.float32)
        * score_scale
    )
    fresh_max = jnp.maximum(run_max, jnp.max(scores, axis=-1))
    rescale = jnp.exp(run_max - fresh_max)
    expo = jnp.exp(scores - fresh_max[..., None])
    denoms = denoms * rescale + jnp.sum(expo, axis=-1)
    numers = numers * rescale[..., None] + jnp.einsum(
        "hqk,hkd->hqd", expo.astype(jnp.bfloat16), value_block, preferred_element_type=jnp.float32
    )
    return (fresh_max, denoms, numers)


def per_device(
    queries,
    keys,
    values,
    norm_gain,
    head_weight,
    head_bias,
    in_weight,
    in_bias,
    conv_weight,
    conv_bias,
):
    frame_dev, rows_dev, cols_dev, feat = queries.shape
    seq_count = lax.axis_size("seq")
    feat_dev = feat // seq_count
    heads_dev = feat_dev // HD
    score_scale = HD ** (-0.5)
    query_all, key_all, value_all = (
        lax.all_to_all(queries, "seq", split_axis=3, concat_axis=1, tiled=True),
        lax.all_to_all(keys, "seq", split_axis=3, concat_axis=1, tiled=True),
        lax.all_to_all(values, "seq", split_axis=3, concat_axis=1, tiled=True),
    )
    all_rows = query_all.shape[1]

    def to_heads(block):
        return block.reshape(-1, heads_dev, HD).transpose(1, 0, 2)

    query_heads = to_heads(query_all)
    key_heads = to_heads(key_all)
    value_heads = to_heads(value_all)
    token_local = query_heads.shape[1]

    def attend_piece(running, block_pair):
        key_piece, value_piece = block_pair
        key_rows = key_piece.shape[1]
        if key_rows > 1024 and key_rows % 1024 == 0:
            count = key_rows // 1024
            key_split = key_piece.reshape(heads_dev, count, 1024, HD).transpose(1, 0, 2, 3)
            value_split = value_piece.reshape(heads_dev, count, 1024, HD).transpose(1, 0, 2, 3)

            def step_block(state, pair_block):
                return (absorb(state, pair_block[0], pair_block[1], query_heads, score_scale), None)

            running, _ = lax.scan(step_block, running, (key_split, value_split))
            return running
        return absorb(running, key_piece, value_piece, query_heads, score_scale)

    start_state = (
        jnp.full((heads_dev, token_local), -1e30, jnp.float32),
        jnp.zeros((heads_dev, token_local), jnp.float32),
        jnp.zeros((heads_dev, token_local, HD), jnp.float32),
    )
    run_max, denoms, numers = attend_piece(
        start_state,
        (
            lax.all_gather(key_heads, ("blk", "chan"), axis=1, tiled=True),
            lax.all_gather(value_heads, ("blk", "chan"), axis=1, tiled=True),
        ),
    )
    attended = (numers / denoms[..., None]).astype(jnp.bfloat16)
    attended = attended.transpose(1, 0, 2).reshape(frame_dev, all_rows, cols_dev, feat_dev)
    back = lax.all_to_all(attended, "seq", split_axis=1, concat_axis=3, tiled=True)
    wide_att = back.astype(jnp.float32)
    squares = jnp.sum(wide_att * wide_att, axis=-1)
    normed = (wide_att * norm_gain).astype(jnp.bfloat16)
    projected = jnp.einsum("frcd,dl->frcl", normed, head_weight, preferred_element_type=jnp.float32)
    rms = jnp.sqrt(squares / feat + epsilon)
    latent_cols = (projected / rms[..., None] + head_bias).astype(jnp.bfloat16)
    latent = lax.all_gather(latent_cols, "chan", axis=2, tiled=True)
    wide_rows = with_halo(latent, (("seq", 1),), 2)
    pre_act = conv_valid(wide_rows, in_weight) + in_bias
    row_ids = lax.axis_index("seq") * rows_dev - 1 + jnp.arange(rows_dev + 2, dtype=jnp.int32)
    inside = (row_ids >= 0) & (row_ids < rows_dev * seq_count)
    activation = jnp.where(inside[None, :, None, None], jax.nn.silu(pre_act), 0.0).astype(
        jnp.bfloat16
    )
    decoded = (conv_valid(activation, conv_weight) + conv_bias).astype(jnp.bfloat16)
    return decoded


def part_kernel(
    sizes,
    q_hbm,
    k_hbm,
    v_hbm,
    gain_hbm,
    head_hbm,
    hbias_hbm,
    win_hbm,
    bin_hbm,
    wconv_hbm,
    bconv_hbm,
    out_ref,
    q_buf,
    k_buf,
    v_buf,
    probs,
    denom,
    stage,
    parts,
    lat_out,
    lat_buf,
    gain,
    head,
    hbias,
    win,
    bin_,
    wconv,
    bconv,
    send_sem,
    recv_sem,
    local_sem,
    part_send,
    part_recv,
    lat_send,
    lat_recv,
):
    seq_count, blk_count, chan_count, feat = sizes
    count = seq_count * blk_count * chan_count
    _, rows_dev, cols_dev, width = q_buf.shape
    heads_dev = width // HD
    tokens_dev = rows_dev * cols_dev
    tokens = count * tokens_dev
    lat = hbias.shape[1]
    seq, blk, chan = lax.axis_index("seq"), lax.axis_index("blk"), lax.axis_index("chan")
    me = (seq * blk_count + blk) * chan_count + chan

    def at_rank(rank):
        return {
            "seq": rank // (blk_count * chan_count),
            "blk": (rank // chan_count) % blk_count,
            "chan": rank % chan_count,
        }

    def ahead(step):
        return lax.rem(me + step, count)

    own = pl.ds(pl.multiple_of(me * width, HD), width)
    locals_ = [
        pltpu.make_async_copy(src, dst, local_sem.at[i])
        for i, (src, dst) in enumerate(
            [
                (q_hbm.at[0, :, :, own], q_buf.at[0]),
                (k_hbm.at[0, :, :, own], k_buf.at[0]),
                (v_hbm.at[0, :, :, own], v_buf.at[0]),
                (gain_hbm.at[:, own], gain),
                (head_hbm.at[own, :], head),
                (hbias_hbm, hbias),
                (win_hbm, win),
                (bin_hbm, bin_),
                (wconv_hbm, wconv),
                (bconv_hbm, bconv),
            ]
        )
    ]

    barrier = pltpu.get_barrier_semaphore()
    for step in range(1, count):
        pl.semaphore_signal(barrier, inc=1, device_id=at_rank(ahead(step)), device_id_type=MESH)
    for copy in locals_:
        copy.start()
    pl.semaphore_wait(barrier, count - 1)

    order = sorted(range(1, count), key=lambda step: abs(step - count / 2))
    tensors = ((q_hbm, q_buf), (k_hbm, k_buf), (v_hbm, v_buf))
    copies = [{}, {}, {}]
    for group in ((0, 1), (2,)):
        for step in order:
            peer = ahead(step)
            columns = pl.ds(pl.multiple_of(peer * width, HD), width)
            for which in group:
                src, dst = tensors[which]
                copy = pltpu.make_async_remote_copy(
                    src_ref=src.at[0, :, :, columns],
                    dst_ref=dst.at[step],
                    send_sem=send_sem.at[which, step],
                    recv_sem=recv_sem.at[which, step],
                    device_id=at_rank(peer),
                    device_id_type=MESH,
                )
                copy.start()
                copies[which][step] = copy

    @pl.when(seq == 0)
    def _():
        lat_buf[0] = jnp.zeros(lat_buf.shape[1:], lat_buf.dtype)

    @pl.when(seq == seq_count - 1)
    def _():
        lat_buf[2] = jnp.zeros(lat_buf.shape[1:], lat_buf.dtype)

    for which in (0, 1):
        locals_[which].wait()
        for step in order:
            copies[which][step].wait_recv()

    slots = max(1, min(count, 128 // tokens_dev))
    while count % slots:
        slots -= 1
    block = slots * tokens_dev
    scale = HD ** (-0.5) * LOG2E
    for head_id in range(heads_dev):
        lanes = slice(head_id * HD, (head_id + 1) * HD)
        key_head = k_buf[:, :, :, lanes].reshape(tokens, HD)
        for start in range(0, count, slots):
            query = q_buf[start : start + slots, :, :, lanes].reshape(block, HD)
            scores = lax.dot_general(
                query, key_head, (((1,), (1,)), ((), ())), preferred_element_type=jnp.float32
            )
            top = jnp.max(scores, axis=-1, keepdims=True)
            expo = jnp.exp2((scores - top) * scale)
            rows = slice(start * tokens_dev, start * tokens_dev + block)
            denom[head_id, rows, :] = jnp.sum(expo, axis=-1, keepdims=True)
            probs[head_id, rows, :] = expo.astype(jnp.bfloat16)

    for index in range(2, len(locals_)):
        locals_[index].wait()
    for step in order:
        copies[2][step].wait_recv()

    lane = lax.broadcasted_iota(jnp.int32, (block, 2 * lat), 1)
    returns = {}
    gain_row = gain[...]
    for start in range(0, count, slots):
        rows = slice(start * tokens_dev, start * tokens_dev + block)
        total = jnp.zeros((block, 2 * lat), jnp.float32)
        squares = jnp.zeros((block, 1), jnp.float32)
        for head_id in range(heads_dev):
            lanes = slice(head_id * HD, (head_id + 1) * HD)
            value_head = v_buf[:, :, :, lanes].reshape(tokens, HD)
            numer = jnp.dot(
                probs[head_id, rows, :], value_head, preferred_element_type=jnp.float32
            )
            attended = (numer / denom[head_id, rows, :]).astype(jnp.bfloat16).astype(jnp.float32)
            squares = squares + jnp.sum(attended * attended, axis=-1, keepdims=True)
            normed = (attended * gain_row[:, lanes]).astype(jnp.bfloat16)
            weight = head[lanes, :]
            both = jnp.concatenate([weight, jnp.zeros_like(weight)], axis=-1)
            total = total + jnp.dot(normed, both, preferred_element_type=jnp.float32)
        high = squares.astype(jnp.bfloat16).astype(jnp.float32)
        packed = jnp.where(
            lane < lat, total, jnp.where(lane < lat + lat // 2, high, squares - high)
        ).astype(jnp.bfloat16)
        stage[start : start + slots] = packed.reshape(slots, rows_dev, cols_dev, 2 * lat)
        for step in range(start, start + slots):
            if step == 0:
                continue
            copy = pltpu.make_async_remote_copy(
                src_ref=stage.at[step],
                dst_ref=parts.at[step],
                send_sem=part_send.at[step],
                recv_sem=part_recv.at[step],
                device_id=at_rank(ahead(count - step)),
                device_id_type=MESH,
            )
            copy.start()
            returns[step] = copy

    for copy in returns.values():
        copy.wait_recv()
    total = stage[0].astype(jnp.float32)
    for step in range(1, count):
        total = total + parts[step].astype(jnp.float32)
    total = total.reshape(tokens_dev, 2 * lat)
    squares = total[:, lat : lat + 1] + total[:, lat + lat // 2 : lat + lat // 2 + 1]
    rms = jnp.sqrt(squares / feat + epsilon)
    low_lane = lax.broadcasted_iota(jnp.int32, total.shape, 1) < lat
    twice = jnp.where(low_lane, total, pltpu.roll(total, lat, 1))
    bias = hbias[...]
    latent = (twice / rms + jnp.concatenate([bias, bias], axis=-1)).astype(jnp.bfloat16)
    latent = latent.reshape(rows_dev, cols_dev, 2 * lat)
    lat_out[...] = latent
    lat_buf[1, chan] = latent

    def lat_copy(shift, turn):
        return pltpu.make_async_remote_copy(
            src_ref=lat_out,
            dst_ref=lat_buf.at[1 - shift, chan],
            send_sem=lat_send.at[1 - shift, turn],
            recv_sem=lat_recv.at[1 - shift, turn],
            device_id={"seq": seq + shift, "blk": blk, "chan": lax.rem(chan + turn, chan_count)},
            device_id_type=MESH,
        )

    def lat_wait(shift, turn):
        source = lax.rem(chan + chan_count - turn, chan_count)
        pltpu.make_async_remote_copy(
            src_ref=lat_out,
            dst_ref=lat_buf.at[1 - shift, source],
            send_sem=lat_send.at[1 - shift, turn],
            recv_sem=lat_recv.at[1 - shift, turn],
            device_id={"seq": seq, "blk": blk, "chan": chan},
            device_id_type=MESH,
        ).wait_recv()

    @pl.when(seq < seq_count - 1)
    def _():
        for turn in range(chan_count):
            lat_copy(1, turn).start()

    @pl.when(seq > 0)
    def _():
        for turn in range(chan_count):
            lat_copy(-1, turn).start()

    for turn in range(1, chan_count):
        lat_copy(0, turn).start()

    for turn in range(1, chan_count):
        lat_wait(0, turn)

    @pl.when(seq > 0)
    def _():
        for turn in range(chan_count):
            lat_wait(1, turn)

    @pl.when(seq < seq_count - 1)
    def _():
        for turn in range(chan_count):
            lat_wait(-1, turn)

    pieces = []
    for side in range(3):
        picked = range(rows_dev - 2, rows_dev) if side == 0 else range(rows_dev if side == 1 else 2)
        for row in picked:
            for part in range(chan_count):
                pieces.append(lat_buf[side, part, row])
    cols = chan_count * cols_dev
    cells = jnp.concatenate(pieces, axis=0).astype(jnp.float32)

    def shifted(cells):
        col = lax.rem(lax.broadcasted_iota(jnp.int32, cells.shape, 0), cols)
        before = jnp.where(col == 0, 0.0, pltpu.roll(cells, 1, 0))
        after = jnp.where(col == cols - 1, 0.0, pltpu.roll(cells, cells.shape[0] - 1, 0))
        return before, after

    before, after = shifted(cells)
    low_lane = lax.broadcasted_iota(jnp.int32, cells.shape, 1) < lat
    stacked = jnp.concatenate(
        [
            jnp.where(low_lane, before, cells).astype(jnp.bfloat16),
            after.astype(jnp.bfloat16)[:, :lat],
        ],
        axis=-1,
    )
    rows_act = rows_dev + 2
    pre_act = jnp.zeros((rows_act * cols, win.shape[3]), jnp.float32)
    for tap in range(3):
        pre_act = pre_act + jnp.dot(
            stacked[tap * cols : (tap + rows_act) * cols],
            win[tap].reshape(3 * lat, win.shape[3]),
            preferred_element_type=jnp.float32,
        )
    pre_act = pre_act + bin_[...]
    row = lax.broadcasted_iota(jnp.int32, pre_act.shape, 0) // cols + (seq * rows_dev - 1)
    inside = (row >= 0) & (row < rows_dev * seq_count)
    activation = jnp.where(inside, pre_act / (1.0 + jnp.exp(-pre_act)), 0.0)
    before, after = shifted(activation)
    taps = [side.astype(jnp.bfloat16) for side in (before, activation, after)]
    result = jnp.zeros((rows_dev * cols, wconv.shape[3]), jnp.float32)
    for tap in range(3):
        for side in range(3):
            result = result + jnp.dot(
                taps[side][tap * cols : (tap + rows_dev) * cols],
                wconv[tap, side],
                preferred_element_type=jnp.float32,
            )
    result = (result + bconv[...]).astype(jnp.bfloat16)
    out_ref[0] = result.reshape(rows_dev, cols, wconv.shape[3])

    for which in range(3):
        for step in order:
            copies[which][step].wait_send()
    for copy in returns.values():
        copy.wait_send()
    for turn in range(1, chan_count):
        lat_copy(0, turn).wait_send()

    @pl.when(seq < seq_count - 1)
    def _():
        for turn in range(chan_count):
            lat_copy(1, turn).wait_send()

    @pl.when(seq > 0)
    def _():
        for turn in range(chan_count):
            lat_copy(-1, turn).wait_send()


def per_device_kernel(
    queries,
    keys,
    values,
    norm_gain,
    head_weight,
    head_bias,
    in_weight,
    in_bias,
    conv_weight,
    conv_bias,
):
    _, rows_dev, cols_dev, feat = queries.shape
    seq_count, blk_count, chan_count = (lax.axis_size(a) for a in ("seq", "blk", "chan"))
    count = seq_count * blk_count * chan_count
    width = feat // count
    tokens_dev = rows_dev * cols_dev
    tokens = count * tokens_dev
    heads_dev = width // HD
    lat = head_weight.shape[1]
    bf16, f32, dma = jnp.bfloat16, jnp.float32, pltpu.SemaphoreType.DMA
    row = lambda vector: vector.reshape(1, -1)
    return pl.pallas_call(
        functools.partial(part_kernel, (seq_count, blk_count, chan_count, feat)),
        out_shape=jax.ShapeDtypeStruct(
            (1, rows_dev, cols_dev * chan_count, conv_weight.shape[3]), bf16
        ),
        in_specs=[pl.BlockSpec(memory_space=pl.ANY)] * 10,
        out_specs=pl.BlockSpec(memory_space=pltpu.VMEM),
        scratch_shapes=[
            pltpu.VMEM((count, rows_dev, cols_dev, width), bf16),
            pltpu.VMEM((count, rows_dev, cols_dev, width), bf16),
            pltpu.VMEM((count, rows_dev, cols_dev, width), bf16),
            pltpu.VMEM((heads_dev, tokens, tokens), bf16),
            pltpu.VMEM((heads_dev, tokens, 1), f32),
            pltpu.VMEM((count, rows_dev, cols_dev, 2 * lat), bf16),
            pltpu.VMEM((count, rows_dev, cols_dev, 2 * lat), bf16),
            pltpu.VMEM((rows_dev, cols_dev, 2 * lat), bf16),
            pltpu.VMEM((3, chan_count, rows_dev, cols_dev, 2 * lat), bf16),
            pltpu.VMEM((1, width), f32),
            pltpu.VMEM((width, lat), bf16),
            pltpu.VMEM((1, lat), f32),
            pltpu.VMEM(in_weight.shape, bf16),
            pltpu.VMEM((1, in_bias.shape[0]), f32),
            pltpu.VMEM(conv_weight.shape, bf16),
            pltpu.VMEM((1, conv_bias.shape[0]), f32),
            dma((3, count)),
            dma((3, count)),
            dma((10,)),
            dma((count,)),
            dma((count,)),
            dma((3, chan_count)),
            dma((3, chan_count)),
        ],
        compiler_params=pltpu.CompilerParams(collective_id=0, has_side_effects=True),
        name="part_kernel",
    )(
        queries,
        keys,
        values,
        row(norm_gain),
        head_weight,
        row(head_bias),
        in_weight,
        row(in_bias),
        conv_weight,
        row(conv_bias),
    )


def fits_kernel(queries, head_weight, mesh):
    frames, rows, cols, feat = queries.shape
    seq_count, blk_count, chan_count = (mesh.shape[a] for a in ("seq", "blk", "chan"))
    count = seq_count * blk_count * chan_count
    return (
        feat % (count * HD) == 0
        and frames == mesh.shape["groups"] * blk_count
        and rows // seq_count >= 2
        and (cols // chan_count) % 16 == 0
        and 2 * head_weight.shape[1] == 128
    )


def solution(mesh):
    def run(*args):
        body = per_device_kernel if fits_kernel(args[0], args[4], mesh) else per_device
        return jax.shard_map(
            body,
            mesh=mesh,
            in_specs=(
                P(("groups", "blk"), "seq", "chan", None),
                P(("groups", "blk"), "seq", "chan", None),
                P(("groups", "blk"), "seq", "chan", None),
                P(),
                P(),
                P(),
                P(),
                P(),
                P(None, None, None, "chan"),
                P("chan"),
            ),
            out_specs=P(("groups", "blk"), "seq", None, "chan"),
            check_vma=False,
        )(*args)

    return run
```

```python
import functools

import jax
import jax.numpy as jnp
from jax import lax
from jax.experimental import pallas as pl
from jax.experimental.pallas import tpu as pltpu
from jax.sharding import PartitionSpec as P

HD = 128
LOG2E = 1.4426950408889634
BLOCK = 128
MESH = pl.DeviceIdType.MESH


epsilon = 1e-06


def with_halo(cells, sides, width):
    for axis, dim in sides:
        count = lax.axis_size(axis)
        ends = count - 1
        head = lax.slice_in_dim(cells, 0, width, axis=dim)
        tail = lax.slice_in_dim(cells, cells.shape[dim] - width, cells.shape[dim], axis=dim)
        cells = jnp.concatenate(
            [
                lax.ppermute(tail, axis, [(i, (i + 1) % count) for i in range(ends)]),
                cells,
                lax.ppermute(head, axis, [((i + 1) % count, i) for i in range(ends)]),
            ],
            axis=dim,
        )
    return cells


def conv_valid(inputs, kernel):
    col_count = inputs.shape[2]
    padded = jnp.pad(inputs, ((0, 0), (0, 0), (1, 1), (0, 0)))
    stacked = jnp.concatenate(
        [padded[:, :, col_tap : col_tap + col_count, :] for col_tap in range(3)], axis=-1
    )
    rows_out = inputs.shape[1] - 2
    result = None
    for row_tap in range(3):
        flat_kernel = kernel[row_tap].reshape(3 * kernel.shape[2], kernel.shape[3])
        term = jnp.einsum(
            "frci,io->frco",
            stacked[:, row_tap : row_tap + rows_out],
            flat_kernel,
            preferred_element_type=jnp.float32,
        )
        result = term if result is None else result + term
    return result


def absorb(running, key_block, value_block, query_heads, score_scale):
    run_max, denoms, numers = running
    scores = (
        jnp.einsum("hqd,hkd->hqk", query_heads, key_block, preferred_element_type=jnp.float32)
        * score_scale
    )
    fresh_max = jnp.maximum(run_max, jnp.max(scores, axis=-1))
    rescale = jnp.exp(run_max - fresh_max)
    expo = jnp.exp(scores - fresh_max[..., None])
    denoms = denoms * rescale + jnp.sum(expo, axis=-1)
    numers = numers * rescale[..., None] + jnp.einsum(
        "hqk,hkd->hqd", expo.astype(jnp.bfloat16), value_block, preferred_element_type=jnp.float32
    )
    return (fresh_max, denoms, numers)


def per_device(
    queries,
    keys,
    values,
    norm_gain,
    head_weight,
    head_bias,
    in_weight,
    in_bias,
    conv_weight,
    conv_bias,
):
    frame_dev, rows_dev, cols_dev, feat = queries.shape
    seq_count = lax.axis_size("seq")
    feat_dev = feat // seq_count
    heads_dev = feat_dev // HD
    score_scale = HD ** (-0.5)
    query_all, key_all, value_all = (
        lax.all_to_all(queries, "seq", split_axis=3, concat_axis=1, tiled=True),
        lax.all_to_all(keys, "seq", split_axis=3, concat_axis=1, tiled=True),
        lax.all_to_all(values, "seq", split_axis=3, concat_axis=1, tiled=True),
    )
    all_rows = query_all.shape[1]

    def to_heads(block):
        return block.reshape(-1, heads_dev, HD).transpose(1, 0, 2)

    query_heads = to_heads(query_all)
    key_heads = to_heads(key_all)
    value_heads = to_heads(value_all)
    token_local = query_heads.shape[1]

    def attend_piece(running, block_pair):
        key_piece, value_piece = block_pair
        key_rows = key_piece.shape[1]
        if key_rows > 1024 and key_rows % 1024 == 0:
            count = key_rows // 1024
            key_split = key_piece.reshape(heads_dev, count, 1024, HD).transpose(1, 0, 2, 3)
            value_split = value_piece.reshape(heads_dev, count, 1024, HD).transpose(1, 0, 2, 3)

            def step_block(state, pair_block):
                return (absorb(state, pair_block[0], pair_block[1], query_heads, score_scale), None)

            running, _ = lax.scan(step_block, running, (key_split, value_split))
            return running
        return absorb(running, key_piece, value_piece, query_heads, score_scale)

    start_state = (
        jnp.full((heads_dev, token_local), -1e30, jnp.float32),
        jnp.zeros((heads_dev, token_local), jnp.float32),
        jnp.zeros((heads_dev, token_local, HD), jnp.float32),
    )
    run_max, denoms, numers = attend_piece(
        start_state,
        (
            lax.all_gather(key_heads, ("blk", "chan"), axis=1, tiled=True),
            lax.all_gather(value_heads, ("blk", "chan"), axis=1, tiled=True),
        ),
    )
    attended = (numers / denoms[..., None]).astype(jnp.bfloat16)
    attended = attended.transpose(1, 0, 2).reshape(frame_dev, all_rows, cols_dev, feat_dev)
    back = lax.all_to_all(attended, "seq", split_axis=1, concat_axis=3, tiled=True)
    wide_att = back.astype(jnp.float32)
    squares = jnp.sum(wide_att * wide_att, axis=-1)
    normed = (wide_att * norm_gain).astype(jnp.bfloat16)
    projected = jnp.einsum("frcd,dl->frcl", normed, head_weight, preferred_element_type=jnp.float32)
    rms = jnp.sqrt(squares / feat + epsilon)
    latent_cols = (projected / rms[..., None] + head_bias).astype(jnp.bfloat16)
    latent = lax.all_gather(latent_cols, "chan", axis=2, tiled=True)
    wide_rows = with_halo(latent, (("seq", 1),), 2)
    pre_act = conv_valid(wide_rows, in_weight) + in_bias
    row_ids = lax.axis_index("seq") * rows_dev - 1 + jnp.arange(rows_dev + 2, dtype=jnp.int32)
    inside = (row_ids >= 0) & (row_ids < rows_dev * seq_count)
    activation = jnp.where(inside[None, :, None, None], jax.nn.silu(pre_act), 0.0).astype(
        jnp.bfloat16
    )
    decoded = (conv_valid(activation, conv_weight) + conv_bias).astype(jnp.bfloat16)
    return decoded


def part_kernel(
    sizes,
    q_hbm,
    k_hbm,
    v_hbm,
    gain_hbm,
    head_hbm,
    hbias_hbm,
    win_hbm,
    bin_hbm,
    wconv_hbm,
    bconv_hbm,
    out_ref,
    q_buf,
    k_buf,
    v_buf,
    stage,
    parts,
    lat_out,
    lat_buf,
    gain,
    head,
    hbias,
    win,
    bin_,
    wconv,
    bconv,
    send_sem,
    recv_sem,
    local_sem,
    part_send,
    part_recv,
    lat_send,
    lat_recv,
    ready,
):
    seq_count, blk_count, chan_count, feat = sizes
    plane = blk_count * chan_count
    count = seq_count * plane
    _, rows_dev, cols_dev, width = q_buf.shape
    heads_dev = width // HD
    tokens_dev = rows_dev * cols_dev
    tokens = count * tokens_dev
    lat = hbias.shape[1]
    seq, blk, chan = lax.axis_index("seq"), lax.axis_index("blk"), lax.axis_index("chan")
    me = (seq * blk_count + blk) * chan_count + chan

    def at_rank(rank):
        return {
            "seq": rank // plane,
            "blk": (rank // chan_count) % blk_count,
            "chan": rank % chan_count,
        }

    near_ends = jnp.minimum(seq, seq_count - 1 - seq)
    upward = jnp.where(seq < seq_count - 1 - seq, 1, -1)

    def by_distance(place):
        paired = place <= 2 * near_ends
        dist = jnp.where(paired, (place + 1) // 2, place - near_ends)
        return dist, jnp.where(paired, 2 * (place % 2) - 1, upward)

    def rank_of(seq_at, turn):
        return seq_at * plane + lax.rem(me % plane + turn, plane)

    own = pl.ds(pl.multiple_of(me * width, HD), width)
    locals_ = [
        pltpu.make_async_copy(src, dst, local_sem.at[i])
        for i, (src, dst) in enumerate(
            [
                (q_hbm.at[0, :, :, own], q_buf.at[me]),
                (k_hbm.at[0, :, :, own], k_buf.at[me]),
                (v_hbm.at[0, :, :, own], v_buf.at[me]),
                (gain_hbm.at[:, own], gain),
                (head_hbm.at[:, own], head),
                (hbias_hbm, hbias),
                (win_hbm, win),
                (bin_hbm, bin_),
                (wconv_hbm, wconv),
                (bconv_hbm, bconv),
            ]
        )
    ]

    barrier = pltpu.get_barrier_semaphore()

    def greet(seq_at, first):
        for turn in range(first, plane):
            pl.semaphore_signal(
                barrier, inc=1, device_id=at_rank(rank_of(seq_at, turn)), device_id_type=MESH
            )

    has_up, has_down = seq < seq_count - 1, seq > 0
    pl.when(has_up)(lambda: greet(seq + 1, 0))
    pl.when(has_down)(lambda: greet(seq - 1, 0))
    greet(seq, 1)
    for copy in locals_:
        copy.start()
    sides = jnp.where(has_up, 1, 0) + jnp.where(has_down, 1, 0)
    pl.semaphore_wait(barrier, plane - 1 + plane * sides)

    def tell(way, dist):
        pl.semaphore_signal(
            ready.at[(way + 1) // 2, dist],
            inc=1,
            device_id={"seq": seq - way, "blk": blk, "chan": chan},
            device_id_type=MESH,
        )

    if seq_count > 2:

        @pl.when(has_up & has_down)
        def _():
            tell(1, 2)
            tell(-1, 2)

    def moved(which, seq_at, turn, slot):
        src, dst = ((q_hbm, q_buf), (k_hbm, k_buf), (v_hbm, v_buf))[which]
        peer = rank_of(seq_at, turn)
        return pltpu.make_async_remote_copy(
            src_ref=src.at[0, :, :, pl.ds(pl.multiple_of(peer * width, HD), width)],
            dst_ref=dst.at[slot],
            send_sem=send_sem.at[which, peer],
            recv_sem=recv_sem.at[which, slot],
            device_id=at_rank(peer),
            device_id_type=MESH,
        )

    places = [(seq, 1)]
    for place in range(1, seq_count):
        dist, way = by_distance(place)
        places.append((seq + dist * way, 0))
    for place, (seq_at, first) in enumerate(places):
        if place >= 2:
            dist, way = by_distance(place)

            @pl.when(dist >= 2)
            def _():
                pl.semaphore_wait(ready.at[(way + 1) // 2, dist], 1)

                @pl.when((seq - way >= 0) & (seq - way < seq_count))
                def _():
                    tell(way, dist + 1)

        for turn in range(first, plane):
            for which in (1, 2):
                moved(which, seq_at, turn, me).start()
    for seq_at, first in places:
        for turn in range(first, plane):
            moved(0, seq_at, turn, me).start()

    @pl.when(seq == 0)
    def _():
        lat_buf[0] = jnp.zeros(lat_buf.shape[1:], lat_buf.dtype)

    @pl.when(seq == seq_count - 1)
    def _():
        lat_buf[2] = jnp.zeros(lat_buf.shape[1:], lat_buf.dtype)

    for copy in locals_:
        copy.wait()
    for seq_at, first in places:
        for turn in range(first, plane):
            for which in (1, 2):
                moved(which, seq_at, turn, rank_of(seq_at, turn)).wait_recv()

    slots = max(1, min(plane, BLOCK // tokens_dev))
    while plane % slots:
        slots -= 1
    block = slots * tokens_dev
    scale = HD ** (-0.5) * LOG2E
    lane = lax.broadcasted_iota(jnp.int32, (block, 2 * lat), 1)
    gain_row = gain[...]

    def attend(seq_at, first, begin):
        start = seq_at * plane + begin
        for slot in range(begin, begin + slots):
            peer = seq_at * plane + slot

            @pl.when(peer != me)
            def _():
                received(q_buf, recv_sem.at[0, peer], peer).wait_recv()

        total = jnp.zeros((block, 2 * lat), jnp.float32)
        squares = jnp.zeros((block, 1), jnp.float32)
        for head_id in range(heads_dev):
            lanes = slice(head_id * HD, (head_id + 1) * HD)
            query = q_buf[pl.ds(start, slots), :, :, lanes].reshape(block, HD)
            key_head = k_buf[:, :, :, lanes].reshape(tokens, HD)
            value_head = v_buf[:, :, :, lanes].reshape(tokens, HD)
            scores = lax.dot_general(
                query, key_head, (((1,), (1,)), ((), ())), preferred_element_type=jnp.float32
            )
            top = jnp.max(scores, axis=-1, keepdims=True)
            expo = jnp.exp2((scores - top) * scale)
            denom = jnp.sum(expo, axis=-1, keepdims=True)
            numer = jnp.dot(
                expo.astype(jnp.bfloat16), value_head, preferred_element_type=jnp.float32
            )
            attended = (numer / denom).astype(jnp.bfloat16).astype(jnp.float32)
            squares = squares + jnp.sum(attended * attended, axis=-1, keepdims=True)
            normed = (attended * gain_row[:, lanes]).astype(jnp.bfloat16)
            weight = head[:, lanes]
            both = jnp.concatenate([weight, jnp.zeros_like(weight)], axis=0)
            total = total + lax.dot_general(
                normed, both, (((1,), (1,)), ((), ())), preferred_element_type=jnp.float32
            )
        high = squares.astype(jnp.bfloat16).astype(jnp.float32)
        packed = jnp.where(
            lane < lat, total, jnp.where(lane < lat + lat // 2, high, squares - high)
        ).astype(jnp.bfloat16)
        stage[pl.ds(start, slots)] = packed.reshape(slots, rows_dev, cols_dev, 2 * lat)
        for slot in range(begin, begin + slots):
            peer = seq_at * plane + slot

            @pl.when(peer != me)
            def _():
                given(peer, me).start()

    def received(buf, sem, peer):
        return pltpu.make_async_remote_copy(
            src_ref=buf.at[me],
            dst_ref=buf.at[peer],
            send_sem=send_sem.at[0, peer],
            recv_sem=sem,
            device_id=at_rank(peer),
            device_id_type=MESH,
        )

    def given(peer, slot):
        return pltpu.make_async_remote_copy(
            src_ref=stage.at[peer],
            dst_ref=parts.at[slot],
            send_sem=part_send.at[peer],
            recv_sem=part_recv.at[slot],
            device_id=at_rank(peer),
            device_id_type=MESH,
        )

    for seq_at, first in places:
        for begin in range(0, plane, slots):
            attend(seq_at, first, begin)

    total = stage[me].astype(jnp.float32)
    for seq_at, first in places:
        for turn in range(first, plane):
            peer = rank_of(seq_at, turn)
            given(peer, peer).wait_recv()
            total = total + parts[peer].astype(jnp.float32)
    total = total.reshape(tokens_dev, 2 * lat)
    squares = total[:, lat : lat + 1] + total[:, lat + lat // 2 : lat + lat // 2 + 1]
    rms = jnp.sqrt(squares / feat + epsilon)
    low_lane = lax.broadcasted_iota(jnp.int32, total.shape, 1) < lat
    twice = jnp.where(low_lane, total, pltpu.roll(total, lat, 1))
    bias = hbias[...]
    latent = (twice / rms + jnp.concatenate([bias, bias], axis=-1)).astype(jnp.bfloat16)
    latent = latent.reshape(rows_dev, cols_dev, 2 * lat)
    lat_out[...] = latent
    lat_buf[1, chan] = latent

    def lat_copy(shift, turn):
        return pltpu.make_async_remote_copy(
            src_ref=lat_out,
            dst_ref=lat_buf.at[1 - shift, chan],
            send_sem=lat_send.at[1 - shift, turn],
            recv_sem=lat_recv.at[1 - shift, turn],
            device_id={"seq": seq + shift, "blk": blk, "chan": lax.rem(chan + turn, chan_count)},
            device_id_type=MESH,
        )

    def lat_wait(shift, turn):
        source = lax.rem(chan + chan_count - turn, chan_count)
        pltpu.make_async_remote_copy(
            src_ref=lat_out,
            dst_ref=lat_buf.at[1 - shift, source],
            send_sem=lat_send.at[1 - shift, turn],
            recv_sem=lat_recv.at[1 - shift, turn],
            device_id={"seq": seq, "blk": blk, "chan": chan},
            device_id_type=MESH,
        ).wait_recv()

    @pl.when(seq < seq_count - 1)
    def _():
        for turn in range(chan_count):
            lat_copy(1, turn).start()

    @pl.when(seq > 0)
    def _():
        for turn in range(chan_count):
            lat_copy(-1, turn).start()

    for turn in range(1, chan_count):
        lat_copy(0, turn).start()

    for turn in range(1, chan_count):
        lat_wait(0, turn)

    @pl.when(seq > 0)
    def _():
        for turn in range(chan_count):
            lat_wait(1, turn)

    @pl.when(seq < seq_count - 1)
    def _():
        for turn in range(chan_count):
            lat_wait(-1, turn)

    pieces = []
    for side in range(3):
        picked = range(rows_dev - 2, rows_dev) if side == 0 else range(rows_dev if side == 1 else 2)
        for row in picked:
            for part in range(chan_count):
                pieces.append(lat_buf[side, part, row])
    cols = chan_count * cols_dev
    cells = jnp.concatenate(pieces, axis=0).astype(jnp.float32)

    def shifted(cells):
        col = lax.rem(lax.broadcasted_iota(jnp.int32, cells.shape, 0), cols)
        before = jnp.where(col == 0, 0.0, pltpu.roll(cells, 1, 0))
        after = jnp.where(col == cols - 1, 0.0, pltpu.roll(cells, cells.shape[0] - 1, 0))
        return before, after

    before, after = shifted(cells)
    low_lane = lax.broadcasted_iota(jnp.int32, cells.shape, 1) < lat
    stacked = jnp.concatenate(
        [
            jnp.where(low_lane, before, cells).astype(jnp.bfloat16),
            after.astype(jnp.bfloat16)[:, :lat],
        ],
        axis=-1,
    )
    rows_act = rows_dev + 2
    pre_act = jnp.zeros((rows_act * cols, win.shape[3]), jnp.float32)
    for tap in range(3):
        pre_act = pre_act + jnp.dot(
            stacked[tap * cols : (tap + rows_act) * cols],
            win[tap].reshape(3 * lat, win.shape[3]),
            preferred_element_type=jnp.float32,
        )
    pre_act = pre_act + bin_[...]
    row = lax.broadcasted_iota(jnp.int32, pre_act.shape, 0) // cols + (seq * rows_dev - 1)
    inside = (row >= 0) & (row < rows_dev * seq_count)
    activation = jnp.where(inside, pre_act / (1.0 + jnp.exp(-pre_act)), 0.0)
    before, after = shifted(activation)
    taps = [side.astype(jnp.bfloat16) for side in (before, activation, after)]
    result = jnp.zeros((rows_dev * cols, wconv.shape[3]), jnp.float32)
    for tap in range(3):
        for side in range(3):
            result = result + jnp.dot(
                taps[side][tap * cols : (tap + rows_dev) * cols],
                wconv[tap, side],
                preferred_element_type=jnp.float32,
            )
    result = (result + bconv[...]).astype(jnp.bfloat16)
    out_ref[0] = result.reshape(rows_dev, cols, wconv.shape[3])

    for seq_at, first in places:
        for turn in range(first, plane):
            peer = rank_of(seq_at, turn)
            for which in range(3):
                moved(which, seq_at, turn, me).wait_send()
            given(peer, me).wait_send()
    for turn in range(1, chan_count):
        lat_copy(0, turn).wait_send()

    @pl.when(seq < seq_count - 1)
    def _():
        for turn in range(chan_count):
            lat_copy(1, turn).wait_send()

    @pl.when(seq > 0)
    def _():
        for turn in range(chan_count):
            lat_copy(-1, turn).wait_send()


def per_device_kernel(
    queries,
    keys,
    values,
    norm_gain,
    head_weight,
    head_bias,
    in_weight,
    in_bias,
    conv_weight,
    conv_bias,
):
    _, rows_dev, cols_dev, feat = queries.shape
    seq_count, blk_count, chan_count = (lax.axis_size(a) for a in ("seq", "blk", "chan"))
    count = seq_count * blk_count * chan_count
    width = feat // count
    lat = head_weight.shape[1]
    bf16, f32, dma = jnp.bfloat16, jnp.float32, pltpu.SemaphoreType.DMA
    row = lambda vector: vector.reshape(1, -1)
    return pl.pallas_call(
        functools.partial(part_kernel, (seq_count, blk_count, chan_count, feat)),
        out_shape=pltpu.VMEM(
            (1, rows_dev, cols_dev * chan_count, conv_weight.shape[3]), bf16
        ),
        in_specs=[pl.BlockSpec(memory_space=pl.ANY)] * 10,
        out_specs=pl.BlockSpec(memory_space=pltpu.VMEM),
        scratch_shapes=[
            pltpu.VMEM((count, rows_dev, cols_dev, width), bf16),
            pltpu.VMEM((count, rows_dev, cols_dev, width), bf16),
            pltpu.VMEM((count, rows_dev, cols_dev, width), bf16),
            pltpu.VMEM((count, rows_dev, cols_dev, 2 * lat), bf16),
            pltpu.VMEM((count, rows_dev, cols_dev, 2 * lat), bf16),
            pltpu.VMEM((rows_dev, cols_dev, 2 * lat), bf16),
            pltpu.VMEM((3, chan_count, rows_dev, cols_dev, 2 * lat), bf16),
            pltpu.VMEM((1, width), f32),
            pltpu.VMEM((lat, width), bf16),
            pltpu.VMEM((1, lat), f32),
            pltpu.VMEM(in_weight.shape, bf16),
            pltpu.VMEM((1, in_bias.shape[0]), f32),
            pltpu.VMEM(conv_weight.shape, bf16),
            pltpu.VMEM((1, conv_bias.shape[0]), f32),
            dma((3, count)),
            dma((3, count)),
            dma((10,)),
            dma((count,)),
            dma((count,)),
            dma((3, chan_count)),
            dma((3, chan_count)),
            pltpu.SemaphoreType.REGULAR((2, seq_count + 1)),
        ],
        compiler_params=pltpu.CompilerParams(collective_id=0, has_side_effects=True),
        name="part_kernel",
    )(
        queries,
        keys,
        values,
        row(norm_gain),
        head_weight.T,
        row(head_bias),
        in_weight,
        row(in_bias),
        conv_weight,
        row(conv_bias),
    )


def fits_kernel(queries, head_weight, mesh):
    frames, rows, cols, feat = queries.shape
    seq_count, blk_count, chan_count = (mesh.shape[a] for a in ("seq", "blk", "chan"))
    count = seq_count * blk_count * chan_count
    return (
        feat % (count * HD) == 0
        and frames == mesh.shape["groups"] * blk_count
        and rows // seq_count >= 2
        and (cols // chan_count) % 16 == 0
        and 2 * head_weight.shape[1] == 128
    )


def solution(mesh):
    def run(*args):
        body = per_device_kernel if fits_kernel(args[0], args[4], mesh) else per_device
        return jax.shard_map(
            body,
            mesh=mesh,
            in_specs=(
                P(("groups", "blk"), "seq", "chan", None),
                P(("groups", "blk"), "seq", "chan", None),
                P(("groups", "blk"), "seq", "chan", None),
                P(),
                P(),
                P(),
                P(),
                P(),
                P(None, None, None, "chan"),
                P("chan"),
            ),
            out_specs=P(("groups", "blk"), "seq", None, "chan"),
            check_vma=False,
        )(*args)

    return run
```

```python
import functools

import jax
import jax.numpy as jnp
from jax import lax
from jax.experimental import pallas as pl
from jax.experimental.pallas import tpu as pltpu
from jax.sharding import PartitionSpec as P

HD = 128
LOG2E = 1.4426950408889634
BLOCK = 128
MESH = pl.DeviceIdType.MESH


epsilon = 1e-06


def with_halo(cells, sides, width):
    for axis, dim in sides:
        count = lax.axis_size(axis)
        ends = count - 1
        head = lax.slice_in_dim(cells, 0, width, axis=dim)
        tail = lax.slice_in_dim(cells, cells.shape[dim] - width, cells.shape[dim], axis=dim)
        cells = jnp.concatenate(
            [
                lax.ppermute(tail, axis, [(i, (i + 1) % count) for i in range(ends)]),
                cells,
                lax.ppermute(head, axis, [((i + 1) % count, i) for i in range(ends)]),
            ],
            axis=dim,
        )
    return cells


def conv_valid(inputs, kernel):
    col_count = inputs.shape[2]
    padded = jnp.pad(inputs, ((0, 0), (0, 0), (1, 1), (0, 0)))
    stacked = jnp.concatenate(
        [padded[:, :, col_tap : col_tap + col_count, :] for col_tap in range(3)], axis=-1
    )
    rows_out = inputs.shape[1] - 2
    result = None
    for row_tap in range(3):
        flat_kernel = kernel[row_tap].reshape(3 * kernel.shape[2], kernel.shape[3])
        term = jnp.einsum(
            "frci,io->frco",
            stacked[:, row_tap : row_tap + rows_out],
            flat_kernel,
            preferred_element_type=jnp.float32,
        )
        result = term if result is None else result + term
    return result


def absorb(running, key_block, value_block, query_heads, score_scale):
    run_max, denoms, numers = running
    scores = (
        jnp.einsum("hqd,hkd->hqk", query_heads, key_block, preferred_element_type=jnp.float32)
        * score_scale
    )
    fresh_max = jnp.maximum(run_max, jnp.max(scores, axis=-1))
    rescale = jnp.exp(run_max - fresh_max)
    expo = jnp.exp(scores - fresh_max[..., None])
    denoms = denoms * rescale + jnp.sum(expo, axis=-1)
    numers = numers * rescale[..., None] + jnp.einsum(
        "hqk,hkd->hqd", expo.astype(jnp.bfloat16), value_block, preferred_element_type=jnp.float32
    )
    return (fresh_max, denoms, numers)


def per_device(
    queries,
    keys,
    values,
    norm_gain,
    head_weight,
    head_bias,
    in_weight,
    in_bias,
    conv_weight,
    conv_bias,
):
    frame_dev, rows_dev, cols_dev, feat = queries.shape
    seq_count = lax.axis_size("seq")
    feat_dev = feat // seq_count
    heads_dev = feat_dev // HD
    score_scale = HD ** (-0.5)
    query_all, key_all, value_all = (
        lax.all_to_all(queries, "seq", split_axis=3, concat_axis=1, tiled=True),
        lax.all_to_all(keys, "seq", split_axis=3, concat_axis=1, tiled=True),
        lax.all_to_all(values, "seq", split_axis=3, concat_axis=1, tiled=True),
    )
    all_rows = query_all.shape[1]

    def to_heads(block):
        return block.reshape(-1, heads_dev, HD).transpose(1, 0, 2)

    query_heads = to_heads(query_all)
    key_heads = to_heads(key_all)
    value_heads = to_heads(value_all)
    token_local = query_heads.shape[1]

    def attend_piece(running, block_pair):
        key_piece, value_piece = block_pair
        key_rows = key_piece.shape[1]
        if key_rows > 1024 and key_rows % 1024 == 0:
            count = key_rows // 1024
            key_split = key_piece.reshape(heads_dev, count, 1024, HD).transpose(1, 0, 2, 3)
            value_split = value_piece.reshape(heads_dev, count, 1024, HD).transpose(1, 0, 2, 3)

            def step_block(state, pair_block):
                return (absorb(state, pair_block[0], pair_block[1], query_heads, score_scale), None)

            running, _ = lax.scan(step_block, running, (key_split, value_split))
            return running
        return absorb(running, key_piece, value_piece, query_heads, score_scale)

    start_state = (
        jnp.full((heads_dev, token_local), -1e30, jnp.float32),
        jnp.zeros((heads_dev, token_local), jnp.float32),
        jnp.zeros((heads_dev, token_local, HD), jnp.float32),
    )
    run_max, denoms, numers = attend_piece(
        start_state,
        (
            lax.all_gather(key_heads, ("blk", "chan"), axis=1, tiled=True),
            lax.all_gather(value_heads, ("blk", "chan"), axis=1, tiled=True),
        ),
    )
    attended = (numers / denoms[..., None]).astype(jnp.bfloat16)
    attended = attended.transpose(1, 0, 2).reshape(frame_dev, all_rows, cols_dev, feat_dev)
    back = lax.all_to_all(attended, "seq", split_axis=1, concat_axis=3, tiled=True)
    wide_att = back.astype(jnp.float32)
    squares = jnp.sum(wide_att * wide_att, axis=-1)
    normed = (wide_att * norm_gain).astype(jnp.bfloat16)
    projected = jnp.einsum("frcd,dl->frcl", normed, head_weight, preferred_element_type=jnp.float32)
    rms = jnp.sqrt(squares / feat + epsilon)
    latent_cols = (projected / rms[..., None] + head_bias).astype(jnp.bfloat16)
    latent = lax.all_gather(latent_cols, "chan", axis=2, tiled=True)
    wide_rows = with_halo(latent, (("seq", 1),), 2)
    pre_act = conv_valid(wide_rows, in_weight) + in_bias
    row_ids = lax.axis_index("seq") * rows_dev - 1 + jnp.arange(rows_dev + 2, dtype=jnp.int32)
    inside = (row_ids >= 0) & (row_ids < rows_dev * seq_count)
    activation = jnp.where(inside[None, :, None, None], jax.nn.silu(pre_act), 0.0).astype(
        jnp.bfloat16
    )
    decoded = (conv_valid(activation, conv_weight) + conv_bias).astype(jnp.bfloat16)
    return decoded


def part_kernel(
    sizes,
    q_hbm,
    k_hbm,
    v_hbm,
    gain_hbm,
    head_hbm,
    hbias_hbm,
    win_hbm,
    bin_hbm,
    wconv_hbm,
    bconv_hbm,
    out_ref,
    q_buf,
    k_buf,
    v_buf,
    stage,
    parts,
    lat_out,
    lat_buf,
    gain,
    head,
    hbias,
    win,
    bin_,
    wconv,
    bconv,
    send_sem,
    recv_sem,
    local_sem,
    part_send,
    part_recv,
    lat_send,
    lat_recv,
    ready,
):
    seq_count, blk_count, chan_count, feat = sizes
    plane = blk_count * chan_count
    count = seq_count * plane
    _, rows_dev, cols_dev, width = q_buf.shape
    heads_dev = width // HD
    tokens_dev = rows_dev * cols_dev
    tokens = count * tokens_dev
    lat = hbias.shape[1]
    seq, blk, chan = lax.axis_index("seq"), lax.axis_index("blk"), lax.axis_index("chan")
    me = (seq * blk_count + blk) * chan_count + chan

    def at_rank(rank):
        return {
            "seq": rank // plane,
            "blk": (rank // chan_count) % blk_count,
            "chan": rank % chan_count,
        }

    near_ends = jnp.minimum(seq, seq_count - 1 - seq)
    upward = jnp.where(seq < seq_count - 1 - seq, 1, -1)

    def by_distance(place):
        paired = place <= 2 * near_ends
        dist = jnp.where(paired, (place + 1) // 2, place - near_ends)
        return dist, jnp.where(paired, upward * (2 * (place % 2) - 1), upward)

    def rank_of(seq_at, turn):
        return seq_at * plane + lax.rem(me % plane + turn, plane)

    own = pl.ds(pl.multiple_of(me * width, HD), width)
    locals_ = [
        pltpu.make_async_copy(src, dst, local_sem.at[i])
        for i, (src, dst) in enumerate(
            [
                (q_hbm.at[0, :, :, own], q_buf.at[me]),
                (k_hbm.at[0, :, :, own], k_buf.at[me]),
                (v_hbm.at[0, :, :, own], v_buf.at[me]),
                (gain_hbm.at[:, own], gain),
                (head_hbm.at[:, own], head),
                (hbias_hbm, hbias),
                (win_hbm, win),
                (bin_hbm, bin_),
                (wconv_hbm, wconv),
                (bconv_hbm, bconv),
            ]
        )
    ]

    barrier = pltpu.get_barrier_semaphore()

    def greet(seq_at, first):
        for turn in range(first, plane):
            pl.semaphore_signal(
                barrier, inc=1, device_id=at_rank(rank_of(seq_at, turn)), device_id_type=MESH
            )

    has_up, has_down = seq < seq_count - 1, seq > 0
    pl.when(has_up)(lambda: greet(seq + 1, 0))
    pl.when(has_down)(lambda: greet(seq - 1, 0))
    greet(seq, 1)
    for copy in locals_:
        copy.start()
    sides = jnp.where(has_up, 1, 0) + jnp.where(has_down, 1, 0)
    pl.semaphore_wait(barrier, plane - 1 + plane * sides)

    def tell(way, dist):
        pl.semaphore_signal(
            ready.at[(way + 1) // 2, dist],
            inc=1,
            device_id={"seq": seq - way, "blk": blk, "chan": chan},
            device_id_type=MESH,
        )

    if seq_count > 2:

        @pl.when(has_up & has_down)
        def _():
            tell(1, 2)
            tell(-1, 2)

    def moved(which, seq_at, turn, slot):
        src, dst = ((q_hbm, q_buf), (k_hbm, k_buf), (v_hbm, v_buf))[which]
        peer = rank_of(seq_at, turn)
        return pltpu.make_async_remote_copy(
            src_ref=src.at[0, :, :, pl.ds(pl.multiple_of(peer * width, HD), width)],
            dst_ref=dst.at[slot],
            send_sem=send_sem.at[which, peer],
            recv_sem=recv_sem.at[which, slot],
            device_id=at_rank(peer),
            device_id_type=MESH,
        )

    places = [(seq, 1)]
    for place in range(1, seq_count):
        dist, way = by_distance(place)
        places.append((seq + dist * way, 0))
    def send(which_ones, group):
        for seq_at, first in group:
            for turn in range(first, plane):
                for which in which_ones:
                    moved(which, seq_at, turn, me).start()

    send((1, 2), places[1:2])
    for place in range(2, seq_count):
        dist, way = by_distance(place)

        @pl.when(dist >= 2)
        def _():
            pl.semaphore_wait(ready.at[(way + 1) // 2, dist], 1)

            @pl.when((seq - way >= 0) & (seq - way < seq_count))
            def _():
                tell(way, dist + 1)

    send((1, 2), places[2:] + places[:1])
    send((0,), places[:1] + places[:0:-1])

    @pl.when(seq == 0)
    def _():
        lat_buf[0] = jnp.zeros(lat_buf.shape[1:], lat_buf.dtype)

    @pl.when(seq == seq_count - 1)
    def _():
        lat_buf[2] = jnp.zeros(lat_buf.shape[1:], lat_buf.dtype)

    for copy in locals_:
        copy.wait()
    for seq_at, first in places:
        for turn in range(first, plane):
            for which in (1, 2):
                moved(which, seq_at, turn, rank_of(seq_at, turn)).wait_recv()

    slots = max(1, min(plane, BLOCK // tokens_dev))
    while plane % slots:
        slots -= 1
    block = slots * tokens_dev
    scale = HD ** (-0.5) * LOG2E
    lane = lax.broadcasted_iota(jnp.int32, (block, 2 * lat), 1)
    gain_row = gain[...]

    def attend(seq_at, first, begin):
        start = seq_at * plane + begin
        for slot in range(begin, begin + slots):
            peer = seq_at * plane + slot

            @pl.when(peer != me)
            def _():
                received(q_buf, recv_sem.at[0, peer], peer).wait_recv()

        total = jnp.zeros((block, 2 * lat), jnp.float32)
        squares = jnp.zeros((block, 1), jnp.float32)
        for head_id in range(heads_dev):
            lanes = slice(head_id * HD, (head_id + 1) * HD)
            query = q_buf[pl.ds(start, slots), :, :, lanes].reshape(block, HD)
            key_head = k_buf[:, :, :, lanes].reshape(tokens, HD)
            value_head = v_buf[:, :, :, lanes].reshape(tokens, HD)
            scores = lax.dot_general(
                query, key_head, (((1,), (1,)), ((), ())), preferred_element_type=jnp.float32
            )
            top = jnp.max(scores, axis=-1, keepdims=True)
            expo = jnp.exp2((scores - top) * scale)
            denom = jnp.sum(expo, axis=-1, keepdims=True)
            numer = jnp.dot(
                expo.astype(jnp.bfloat16), value_head, preferred_element_type=jnp.float32
            )
            attended = (numer / denom).astype(jnp.bfloat16).astype(jnp.float32)
            squares = squares + jnp.sum(attended * attended, axis=-1, keepdims=True)
            normed = (attended * gain_row[:, lanes]).astype(jnp.bfloat16)
            weight = head[:, lanes]
            both = jnp.concatenate([weight, jnp.zeros_like(weight)], axis=0)
            total = total + lax.dot_general(
                normed, both, (((1,), (1,)), ((), ())), preferred_element_type=jnp.float32
            )
        high = squares.astype(jnp.bfloat16).astype(jnp.float32)
        packed = jnp.where(
            lane < lat, total, jnp.where(lane < lat + lat // 2, high, squares - high)
        ).astype(jnp.bfloat16)
        stage[pl.ds(start, slots)] = packed.reshape(slots, rows_dev, cols_dev, 2 * lat)
        for slot in range(begin, begin + slots):
            peer = seq_at * plane + slot

            @pl.when(peer != me)
            def _():
                given(peer, me).start()

    def received(buf, sem, peer):
        return pltpu.make_async_remote_copy(
            src_ref=buf.at[me],
            dst_ref=buf.at[peer],
            send_sem=send_sem.at[0, peer],
            recv_sem=sem,
            device_id=at_rank(peer),
            device_id_type=MESH,
        )

    def given(peer, slot):
        return pltpu.make_async_remote_copy(
            src_ref=stage.at[peer],
            dst_ref=parts.at[slot],
            send_sem=part_send.at[peer],
            recv_sem=part_recv.at[slot],
            device_id=at_rank(peer),
            device_id_type=MESH,
        )

    for seq_at, first in places:
        for begin in range(0, plane, slots):
            attend(seq_at, first, begin)

    total = stage[me].astype(jnp.float32)
    for seq_at, first in places:
        for turn in range(first, plane):
            peer = rank_of(seq_at, turn)
            given(peer, peer).wait_recv()
            total = total + parts[peer].astype(jnp.float32)
    total = total.reshape(tokens_dev, 2 * lat)
    squares = total[:, lat : lat + 1] + total[:, lat + lat // 2 : lat + lat // 2 + 1]
    rms = jnp.sqrt(squares / feat + epsilon)
    low_lane = lax.broadcasted_iota(jnp.int32, total.shape, 1) < lat
    twice = jnp.where(low_lane, total, pltpu.roll(total, lat, 1))
    bias = hbias[...]
    latent = (twice / rms + jnp.concatenate([bias, bias], axis=-1)).astype(jnp.bfloat16)
    latent = latent.reshape(rows_dev, cols_dev, 2 * lat)
    lat_out[...] = latent
    lat_buf[1, chan] = latent

    def lat_copy(shift, turn):
        return pltpu.make_async_remote_copy(
            src_ref=lat_out,
            dst_ref=lat_buf.at[1 - shift, chan],
            send_sem=lat_send.at[1 - shift, turn],
            recv_sem=lat_recv.at[1 - shift, turn],
            device_id={"seq": seq + shift, "blk": blk, "chan": lax.rem(chan + turn, chan_count)},
            device_id_type=MESH,
        )

    def lat_wait(shift, turn):
        source = lax.rem(chan + chan_count - turn, chan_count)
        pltpu.make_async_remote_copy(
            src_ref=lat_out,
            dst_ref=lat_buf.at[1 - shift, source],
            send_sem=lat_send.at[1 - shift, turn],
            recv_sem=lat_recv.at[1 - shift, turn],
            device_id={"seq": seq, "blk": blk, "chan": chan},
            device_id_type=MESH,
        ).wait_recv()

    @pl.when(seq < seq_count - 1)
    def _():
        for turn in range(chan_count):
            lat_copy(1, turn).start()

    @pl.when(seq > 0)
    def _():
        for turn in range(chan_count):
            lat_copy(-1, turn).start()

    for turn in range(1, chan_count):
        lat_copy(0, turn).start()

    for turn in range(1, chan_count):
        lat_wait(0, turn)

    @pl.when(seq > 0)
    def _():
        for turn in range(chan_count):
            lat_wait(1, turn)

    @pl.when(seq < seq_count - 1)
    def _():
        for turn in range(chan_count):
            lat_wait(-1, turn)

    pieces = []
    for side in range(3):
        picked = range(rows_dev - 2, rows_dev) if side == 0 else range(rows_dev if side == 1 else 2)
        for row in picked:
            for part in range(chan_count):
                pieces.append(lat_buf[side, part, row])
    cols = chan_count * cols_dev
    cells = jnp.concatenate(pieces, axis=0).astype(jnp.float32)

    def shifted(cells):
        col = lax.rem(lax.broadcasted_iota(jnp.int32, cells.shape, 0), cols)
        before = jnp.where(col == 0, 0.0, pltpu.roll(cells, 1, 0))
        after = jnp.where(col == cols - 1, 0.0, pltpu.roll(cells, cells.shape[0] - 1, 0))
        return before, after

    before, after = shifted(cells)
    low_lane = lax.broadcasted_iota(jnp.int32, cells.shape, 1) < lat
    stacked = jnp.concatenate(
        [
            jnp.where(low_lane, before, cells).astype(jnp.bfloat16),
            after.astype(jnp.bfloat16)[:, :lat],
        ],
        axis=-1,
    )
    rows_act = rows_dev + 2
    pre_act = jnp.zeros((rows_act * cols, win.shape[3]), jnp.float32)
    for tap in range(3):
        pre_act = pre_act + jnp.dot(
            stacked[tap * cols : (tap + rows_act) * cols],
            win[tap].reshape(3 * lat, win.shape[3]),
            preferred_element_type=jnp.float32,
        )
    pre_act = pre_act + bin_[...]
    row = lax.broadcasted_iota(jnp.int32, pre_act.shape, 0) // cols + (seq * rows_dev - 1)
    inside = (row >= 0) & (row < rows_dev * seq_count)
    activation = jnp.where(inside, pre_act / (1.0 + jnp.exp(-pre_act)), 0.0)
    before, after = shifted(activation)
    taps = [side.astype(jnp.bfloat16) for side in (before, activation, after)]
    result = jnp.zeros((rows_dev * cols, wconv.shape[3]), jnp.float32)
    for tap in range(3):
        for side in range(3):
            result = result + jnp.dot(
                taps[side][tap * cols : (tap + rows_dev) * cols],
                wconv[tap, side],
                preferred_element_type=jnp.float32,
            )
    result = (result + bconv[...]).astype(jnp.bfloat16)
    out_ref[0] = result.reshape(rows_dev, cols, wconv.shape[3])

    for seq_at, first in places:
        for turn in range(first, plane):
            peer = rank_of(seq_at, turn)
            for which in range(3):
                moved(which, seq_at, turn, me).wait_send()
            given(peer, me).wait_send()
    for turn in range(1, chan_count):
        lat_copy(0, turn).wait_send()

    @pl.when(seq < seq_count - 1)
    def _():
        for turn in range(chan_count):
            lat_copy(1, turn).wait_send()

    @pl.when(seq > 0)
    def _():
        for turn in range(chan_count):
            lat_copy(-1, turn).wait_send()


def per_device_kernel(
    queries,
    keys,
    values,
    norm_gain,
    head_weight,
    head_bias,
    in_weight,
    in_bias,
    conv_weight,
    conv_bias,
):
    _, rows_dev, cols_dev, feat = queries.shape
    seq_count, blk_count, chan_count = (lax.axis_size(a) for a in ("seq", "blk", "chan"))
    count = seq_count * blk_count * chan_count
    width = feat // count
    lat = head_weight.shape[1]
    bf16, f32, dma = jnp.bfloat16, jnp.float32, pltpu.SemaphoreType.DMA
    row = lambda vector: vector.reshape(1, -1)
    return pl.pallas_call(
        functools.partial(part_kernel, (seq_count, blk_count, chan_count, feat)),
        out_shape=pltpu.VMEM(
            (1, rows_dev, cols_dev * chan_count, conv_weight.shape[3]), bf16
        ),
        in_specs=[pl.BlockSpec(memory_space=pl.ANY)] * 10,
        out_specs=pl.BlockSpec(memory_space=pltpu.VMEM),
        scratch_shapes=[
            pltpu.VMEM((count, rows_dev, cols_dev, width), bf16),
            pltpu.VMEM((count, rows_dev, cols_dev, width), bf16),
            pltpu.VMEM((count, rows_dev, cols_dev, width), bf16),
            pltpu.VMEM((count, rows_dev, cols_dev, 2 * lat), bf16),
            pltpu.VMEM((count, rows_dev, cols_dev, 2 * lat), bf16),
            pltpu.VMEM((rows_dev, cols_dev, 2 * lat), bf16),
            pltpu.VMEM((3, chan_count, rows_dev, cols_dev, 2 * lat), bf16),
            pltpu.VMEM((1, width), f32),
            pltpu.VMEM((lat, width), bf16),
            pltpu.VMEM((1, lat), f32),
            pltpu.VMEM(in_weight.shape, bf16),
            pltpu.VMEM((1, in_bias.shape[0]), f32),
            pltpu.VMEM(conv_weight.shape, bf16),
            pltpu.VMEM((1, conv_bias.shape[0]), f32),
            dma((3, count)),
            dma((3, count)),
            dma((10,)),
            dma((count,)),
            dma((count,)),
            dma((3, chan_count)),
            dma((3, chan_count)),
            pltpu.SemaphoreType.REGULAR((2, seq_count + 1)),
        ],
        compiler_params=pltpu.CompilerParams(collective_id=0, has_side_effects=True),
        name="part_kernel",
    )(
        queries,
        keys,
        values,
        row(norm_gain),
        head_weight.T,
        row(head_bias),
        in_weight,
        row(in_bias),
        conv_weight,
        row(conv_bias),
    )


def fits_kernel(queries, head_weight, mesh):
    frames, rows, cols, feat = queries.shape
    seq_count, blk_count, chan_count = (mesh.shape[a] for a in ("seq", "blk", "chan"))
    count = seq_count * blk_count * chan_count
    return (
        feat % (count * HD) == 0
        and frames == mesh.shape["groups"] * blk_count
        and rows // seq_count >= 2
        and (cols // chan_count) % 16 == 0
        and 2 * head_weight.shape[1] == 128
    )


def solution(mesh):
    def run(*args):
        body = per_device_kernel if fits_kernel(args[0], args[4], mesh) else per_device
        return jax.shard_map(
            body,
            mesh=mesh,
            in_specs=(
                P(("groups", "blk"), "seq", "chan", None),
                P(("groups", "blk"), "seq", "chan", None),
                P(("groups", "blk"), "seq", "chan", None),
                P(),
                P(),
                P(),
                P(),
                P(),
                P(None, None, None, "chan"),
                P("chan"),
            ),
            out_specs=P(("groups", "blk"), "seq", None, "chan"),
            check_vma=False,
        )(*args)

    return run
```
